32 devices in a mesh: row: 8 (over y, x, core), col: 4 (over z).
Axes of the slice: x: 2, y: 2, z: 4, core: 2. Of those that a mesh axis runs over, the one named last changes fastest.
Arguments:
- descriptors: bfloat16 [32, 6144], P(None, ('row', 'col')), may hold values from -6 to 6
- densities: float32 [6144], P(('row', 'col')), may hold values from 0.25 to 4
- vectors: float32 [32, 6144], P(None, ('row', 'col')), may hold values from -6 to 6
Outputs:
- next_block: float32 [32, 6144], P(None, ('row', 'col'))
The draws below stay inside these ranges and needn't reach their ends.
All inputs are finite; a program needn't handle non-finite values.
Results may differ from the reference program's by a relative error of at most 0.0036.
Values may be sent and summed in bfloat16 or wider, within the bound.
No kernel may reach another device: no remote copies, remote signals or barrier semaphores. Data moves between devices by JAX's collectives and lax.ppermute only.
A program may use at most 64 MiB of HBM per device.

```python
import math
import jax
import jax.numpy as jnp
from jax import lax

FEAT = 32
VECS = 32
SAMPLES = 6144


def levels(rng, shape, cuts, smallest, high):
    factor_of = 1.0
    for dim, shards_of in cuts:
        heights = jax.random.uniform(jax.random.fold_in(jax.random.fold_in(rng, 6), dim), (shards_of,), jnp.float32, smallest / len(cuts), high / len(cuts))
        factor_of = factor_of * jnp.repeat(jnp.exp(heights), shape[dim] // shards_of).reshape((-1,) + (1,) * (len(shape) - 1 - dim))
    return factor_of


def normal_values(own_key, dims, scale, limit, cuts=(), held_as=jnp.bfloat16):
    values = jax.random.normal(own_key, dims, jnp.float32) * scale
    if len(cuts) > 0:
        values = levels(own_key, dims, cuts, -0.22, 0.18) * values
    return jnp.clip(values, min=-limit, max=limit).astype(held_as)


def setup_inputs(seed: int = 0) -> dict:
    key_list = jax.random.split(jax.random.key(seed), 4)
    return {
        "descriptors": normal_values(key_list[0], (FEAT, SAMPLES), 1.0, 6.0, ((1, 32),)),
        "densities": jnp.clip(jnp.exp(math.log(4.0) - 2.7725887 * jax.random.uniform(key_list[1], (SAMPLES,), jnp.float32) ** levels(key_list[1], (SAMPLES,), ((0, 32),), -0.2, 0.2)), 0.25, 4.0),
        "vectors": normal_values(key_list[2], (VECS, SAMPLES), 1.0, 6.0, ((1, 32),), jnp.float32),
    }


kernel_width = 8.0

def reference(descriptors, densities, vectors):
    highest = lax.Precision.HIGHEST
    features = descriptors.astype(jnp.float32)
    sq_norms = lax.optimization_barrier(jnp.sum(features * features, axis=0))
    weighted = (vectors / densities[None, :]).astype(jnp.bfloat16).astype(jnp.float32)
    inverse = (1.0 / densities).astype(jnp.bfloat16).astype(jnp.float32)[None, :]
    block_rows = math.gcd(SAMPLES, 1024)
    block_count = SAMPLES // block_rows
    blocked = features.reshape(FEAT, block_count, block_rows).transpose(1, 0, 2)
    norm_blocks = sq_norms.reshape(block_count, block_rows)

    def row_block(block_item):
        block_feat, block_norm = block_item
        inner_prod = jnp.dot(block_feat.T.astype(jnp.float32), features.astype(jnp.float32), precision=highest, preferred_element_type=jnp.float32)
        kernel = jnp.exp(-(block_norm[:, None] + sq_norms[None, :] - 2.0 * inner_prod) / kernel_width)
        kernel = kernel.astype(jnp.bfloat16).astype(jnp.float32)
        numerator = jnp.dot(weighted.astype(jnp.float32), kernel.T.astype(jnp.float32), precision=highest, preferred_element_type=jnp.float32)
        degree = jnp.dot(inverse.astype(jnp.float32), kernel.T.astype(jnp.float32), precision=highest, preferred_element_type=jnp.float32)
        return numerator / degree
    diffused = lax.map(row_block, (blocked, norm_blocks))
    diffused = diffused.transpose(1, 0, 2).reshape(VECS, SAMPLES)
    coupling = jnp.dot(vectors, diffused.T, precision=highest)
    remainder = diffused - jnp.dot(coupling.T, vectors, precision=highest) / SAMPLES
    spread = jnp.dot(remainder, remainder.T, precision=highest)
    factor = jnp.linalg.cholesky(spread)
    solved = jax.scipy.linalg.solve_triangular(factor, remainder, lower=True)
    return math.sqrt(SAMPLES) * solved
```

```python
import functools
import math

import jax
import jax.numpy as jnp
from jax import lax
from jax.experimental import pallas as pl
from jax.experimental.pallas import tpu as pltpu
from jax.sharding import PartitionSpec as P

kernel_width = 8.0
both_axes = ("row", "col")
highest = lax.Precision.HIGHEST
f32 = jnp.float32
bf16 = jnp.bfloat16
pad_rows = 8


def dot(a, b, contract, precision=None):
    return lax.dot_general(
        a, b, (contract, ((), ())), precision=precision, preferred_element_type=f32
    )


def split3(x):
    high = x.astype(bf16)
    rest = x - high.astype(f32)
    mid = rest.astype(bf16)
    low = (rest - mid.astype(f32)).astype(bf16)
    return high.astype(f32), mid.astype(f32), low.astype(f32)


def pack_kernel(desc_ref, dens_ref, vec_ref, out_ref):
    feat, count = desc_ref.shape
    vecs = vec_ref.shape[0]
    half = count // 3
    width = 2 * half
    desc = desc_ref[...]
    dens = dens_ref[...]
    weighted = (vec_ref[...] / dens).astype(bf16)
    inverse = (1.0 / dens).astype(bf16)
    out_ref[0:feat, :] = desc[:, :width]
    out_ref[feat : feat + vecs, :] = weighted[:, :width]
    base = feat + vecs
    out_ref[base : base + feat, :] = jnp.concatenate(
        [desc[:, width:], weighted[:, width:]], axis=1
    )
    base = base + feat
    tail = jnp.concatenate([inverse[:, width:], jnp.zeros((1, half), bf16)], axis=1)
    out_ref[base : base + pad_rows, :] = jnp.concatenate(
        [inverse[:, :width], tail, jnp.zeros((pad_rows - 2, width), bf16)], axis=0
    )


def target_rows(desc):
    values = desc.astype(f32)
    norm = jnp.sum(values * values, axis=0, keepdims=True)
    scale = -1.0 / kernel_width
    high, mid, low = split3(norm)
    ones = jnp.full_like(norm, scale)
    extra = jnp.concatenate(
        [ones, ones, ones, high * scale, mid * scale, low * scale, ones * 0.0, ones * 0.0],
        axis=0,
    )
    stacked = jnp.concatenate([values * (2.0 / kernel_width), extra], axis=0)
    return stacked.T.astype(bf16)


def source_columns(desc):
    values = desc.astype(f32)
    norm = jnp.sum(values * values, axis=0, keepdims=True)
    high, mid, low = split3(norm)
    ones = jnp.ones_like(norm)
    return jnp.concatenate(
        [values, high, mid, low, ones, ones, ones, ones * 0.0, ones * 0.0], axis=0
    ).astype(bf16)


def sums_kernel(packed_ref, own_ref, other_ref, own_out, other_out, *, vecs):
    feat, count = own_ref.shape
    pieces, _, width = packed_ref.shape
    half = count // 3
    rows = jnp.concatenate([target_rows(own_ref[...]), target_rows(other_ref[...])], axis=0)

    def step(pair, total):
        a = packed_ref[2 * pair]
        b = packed_ref[2 * pair + 1]
        base = feat + vecs
        desc = jnp.concatenate(
            [a[:feat], b[:feat], a[base : base + feat, :half], b[base : base + feat, :half]],
            axis=1,
        )
        weighted = jnp.concatenate(
            [a[feat:base], b[feat:base], a[base : base + feat, half:], b[base : base + feat, half:]],
            axis=1,
        )
        base = base + feat
        inverse = jnp.concatenate(
            [
                a[base : base + 1],
                b[base : base + 1],
                a[base + 1 : base + 2, :half],
                b[base + 1 : base + 2, :half],
            ],
            axis=1,
        )
        values = jnp.concatenate(
            [weighted.astype(f32), inverse.astype(f32), jnp.zeros((7, 2 * count), f32)], axis=0
        ).astype(bf16)
        exponent = dot(rows, source_columns(desc), ((1,), (0,)))
        kernel = jnp.exp(exponent).astype(bf16)
        return total + dot(kernel, values, ((1,), (1,)))

    total = lax.fori_loop(
        0, pieces // 2, step, jnp.zeros((2 * count, vecs + 8), f32), unroll=pieces <= 16
    )
    own_out[...] = total[:count].T
    other_out[...] = total[count:].T


def fold(matrix):
    side = matrix.shape[0]
    step = side // 4
    return jnp.concatenate([matrix[i * step : (i + 1) * step] for i in range(4)], axis=1)


def unfold(folded):
    step, width = folded.shape
    side = width // 4
    return jnp.concatenate([folded[:, i * side : (i + 1) * side] for i in range(4)], axis=0)


def gram_kernel(own_ref, got_ref, vec_ref, diffused_out, gram_out):
    vecs = vec_ref.shape[0]
    total = own_ref[...] + got_ref[...]
    diffused = total[:vecs] / total[vecs : vecs + 1]
    vectors = vec_ref[...]
    diffused_out[...] = diffused
    contract = ((1,), (1,))
    coupling = dot(vectors, diffused, contract, highest)
    diffused_gram = dot(diffused, diffused, contract, highest)
    basis_gram = dot(vectors, vectors, contract, highest)
    gram_out[...] = jnp.concatenate(
        [fold(coupling), fold(diffused_gram), fold(basis_gram)], axis=0
    )


def whiten_kernel(gram_ref, diffused_ref, vec_ref, out_ref, *, samples):
    vecs = vec_ref.shape[0]
    step = vecs // 4
    grams = gram_ref[...]
    coupling = unfold(grams[:step])
    diffused_gram = unfold(grams[step : 2 * step])
    basis_gram = unfold(grams[2 * step :])
    inner = dot(basis_gram, coupling, ((1,), (0,)), highest)
    mixed = (2.0 * coupling - inner / samples) / samples
    spread = diffused_gram - dot(coupling, mixed, ((0,), (0,)), highest)
    remainder = diffused_ref[...] - dot(coupling, vec_ref[...], ((0,), (0,)), highest) / samples
    table = spread
    solved = remainder
    row_index = lax.broadcasted_iota(jnp.int32, (vecs, 1), 0)
    for k in range(vecs):
        scale = lax.rsqrt(table[k : k + 1, k : k + 1])
        column = table[:, k : k + 1] * scale
        table_row = table[k : k + 1] * scale
        solved_row = solved[k : k + 1] * scale
        below = row_index > k
        at = row_index == k
        column = jnp.where(below, column, 0.0)
        table = table - column * table_row
        solved = jnp.where(at, solved_row, solved - column * solved_row)
    out_ref[...] = math.sqrt(samples) * solved


def whole(*shape_types):
    outs = tuple(jax.ShapeDtypeStruct(s, t) for s, t in shape_types)
    return outs if len(outs) > 1 else outs[0]


def local_call(body, outs, name, cost):
    return pl.pallas_call(
        body,
        out_shape=outs,
        name=name,
        cost_estimate=pl.CostEstimate(flops=cost, bytes_accessed=cost // 64, transcendentals=0),
    )


def per_device(rows, cols, descriptors, densities, vectors):
    feat, count = descriptors.shape
    vecs = vectors.shape[0]
    samples = float(count * rows * cols)
    devices = rows * cols

    def swap(x, mask):
        return lax.ppermute(x, both_axes, [(i, i ^ mask) for i in range(devices)])

    core_mask = cols
    col_masks = [1 << b for b in range(int(math.log2(cols)))]
    row_masks = [cols << b for b in range(1, int(math.log2(rows)))]
    width = 2 * (count // 3)
    height = 2 * feat + vecs + pad_rows

    other_desc = swap(descriptors, core_mask)
    packed = local_call(pack_kernel, whole(((height, width), bf16)), "pack", 1 << 16)(
        descriptors, densities[None, :], vectors
    )[None]
    for mask in col_masks[::-1] + row_masks:
        packed = jnp.concatenate([packed, swap(packed, mask)], axis=0)
    part = ((vecs + 8, count), f32)
    own, other = local_call(
        functools.partial(sums_kernel, vecs=vecs), whole(part, part), "sums", 1 << 30
    )(packed, descriptors, other_desc)
    got = swap(other, core_mask)
    diffused, grams = local_call(
        gram_kernel,
        whole(((vecs, count), f32), ((3 * vecs // 4, 4 * vecs), f32)),
        "gram",
        1 << 20,
    )(own, got, vectors)
    for mask in [core_mask] + row_masks + col_masks:
        grams = grams + swap(grams, mask)
    return local_call(
        functools.partial(whiten_kernel, samples=samples),
        whole(((vecs, count), f32)),
        "whiten",
        1 << 20,
    )(grams, diffused, vectors)


def solution(mesh):
    rows, cols = mesh.shape["row"], mesh.shape["col"]
    return jax.shard_map(
        functools.partial(per_device, rows, cols),
        mesh=mesh,
        in_specs=(P(None, both_axes), P(both_axes), P(None, both_axes)),
        out_specs=P(None, both_axes),
        check_vma=False,
    )
```

```python
import functools
import math

import jax
import jax.numpy as jnp
from jax import lax
from jax.experimental import pallas as pl
from jax.experimental.pallas import tpu as pltpu
from jax.sharding import PartitionSpec as P

kernel_width = 8.0
both_axes = ("row", "col")
highest = lax.Precision.HIGHEST
f32 = jnp.float32
bf16 = jnp.bfloat16
pad_rows = 8


def dot(a, b, contract, precision=None):
    return lax.dot_general(
        a, b, (contract, ((), ())), precision=precision, preferred_element_type=f32
    )


def split3(x):
    high = x.astype(bf16)
    rest = x - high.astype(f32)
    mid = rest.astype(bf16)
    low = (rest - mid.astype(f32)).astype(bf16)
    return high.astype(f32), mid.astype(f32), low.astype(f32)


def pack_kernel(desc_ref, dens_ref, vec_ref, out_ref):
    feat, count = desc_ref.shape
    vecs = vec_ref.shape[0]
    half = count // 3
    width = 2 * half
    desc = desc_ref[...]
    dens = dens_ref[...]
    weighted = (vec_ref[...] / dens).astype(bf16)
    inverse = (1.0 / dens).astype(bf16)
    out_ref[0:feat, :] = desc[:, :width]
    out_ref[feat : feat + vecs, :] = weighted[:, :width]
    base = feat + vecs
    out_ref[base : base + feat, :] = jnp.concatenate(
        [desc[:, width:], weighted[:, width:]], axis=1
    )
    base = base + feat
    tail = jnp.concatenate([inverse[:, width:], jnp.zeros((1, half), bf16)], axis=1)
    out_ref[base : base + pad_rows, :] = jnp.concatenate(
        [inverse[:, :width], tail, jnp.zeros((pad_rows - 2, width), bf16)], axis=0
    )


def target_rows(desc):
    values = desc.astype(f32)
    norm = jnp.sum(values * values, axis=0, keepdims=True)
    scale = -1.0 / kernel_width
    high, mid, low = split3(norm)
    ones = jnp.full_like(norm, scale)
    extra = jnp.concatenate(
        [ones, ones, ones, high * scale, mid * scale, low * scale, ones * 0.0, ones * 0.0],
        axis=0,
    )
    stacked = jnp.concatenate([values * (2.0 / kernel_width), extra], axis=0)
    return stacked.T.astype(bf16)


def source_columns(desc):
    values = desc.astype(f32)
    norm = jnp.sum(values * values, axis=0, keepdims=True)
    high, mid, low = split3(norm)
    ones = jnp.ones_like(norm)
    return jnp.concatenate(
        [values, high, mid, low, ones, ones, ones, ones * 0.0, ones * 0.0], axis=0
    ).astype(bf16)


def sums_kernel(packed_ref, own_ref, other_ref, own_out, other_out, *, vecs):
    feat, count = own_ref.shape
    pieces, _, width = packed_ref.shape
    half = count // 3
    rows = jnp.concatenate([target_rows(own_ref[...]), target_rows(other_ref[...])], axis=0)

    def step(pair, total):
        a = packed_ref[2 * pair]
        b = packed_ref[2 * pair + 1]
        base = feat + vecs
        desc = jnp.concatenate(
            [a[:feat], b[:feat], a[base : base + feat, :half], b[base : base + feat, :half]],
            axis=1,
        )
        weighted = jnp.concatenate(
            [a[feat:base], b[feat:base], a[base : base + feat, half:], b[base : base + feat, half:]],
            axis=1,
        )
        base = base + feat
        inverse = jnp.concatenate(
            [
                a[base : base + 1],
                b[base : base + 1],
                a[base + 1 : base + 2, :half],
                b[base + 1 : base + 2, :half],
            ],
            axis=1,
        )
        values = jnp.concatenate(
            [weighted.astype(f32), inverse.astype(f32), jnp.zeros((7, 2 * count), f32)], axis=0
        ).astype(bf16)
        exponent = dot(rows, source_columns(desc), ((1,), (0,)))
        kernel = jnp.exp(exponent).astype(bf16)
        return total + dot(kernel, values, ((1,), (1,)))

    total = lax.fori_loop(
        0, pieces // 2, step, jnp.zeros((2 * count, vecs + 8), f32), unroll=pieces <= 16
    )
    own_out[...] = total[:count].T
    other_out[...] = total[count:].T


def fold(matrix):
    side = matrix.shape[0]
    step = side // 4
    return jnp.concatenate([matrix[i * step : (i + 1) * step] for i in range(4)], axis=1)


def unfold(folded):
    step, width = folded.shape
    side = width // 4
    return jnp.concatenate([folded[:, i * side : (i + 1) * side] for i in range(4)], axis=0)


def gram_kernel(own_ref, got_ref, vec_ref, diffused_out, gram_out):
    vecs = vec_ref.shape[0]
    total = own_ref[...] + got_ref[...]
    diffused = total[:vecs] / total[vecs : vecs + 1]
    vectors = vec_ref[...]
    diffused_out[...] = diffused
    contract = ((1,), (1,))
    coupling = dot(vectors, diffused, contract, highest)
    diffused_gram = dot(diffused, diffused, contract, highest)
    basis_gram = dot(vectors, vectors, contract, highest)
    gram_out[...] = jnp.concatenate(
        [fold(coupling), fold(diffused_gram), fold(basis_gram)], axis=0
    )


def whiten_kernel(gram_ref, diffused_ref, vec_ref, out_ref, *, samples):
    vecs = vec_ref.shape[0]
    step = vecs // 4
    grams = gram_ref[...]
    coupling = unfold(grams[:step])
    diffused_gram = unfold(grams[step : 2 * step])
    basis_gram = unfold(grams[2 * step :])
    inner = dot(basis_gram, coupling, ((1,), (0,)), highest)
    mixed = (2.0 * coupling - inner / samples) / samples
    spread = diffused_gram - dot(coupling, mixed, ((0,), (0,)), highest)
    remainder = diffused_ref[...] - dot(coupling, vec_ref[...], ((0,), (0,)), highest) / samples
    table = spread
    solved = remainder
    row_index = lax.broadcasted_iota(jnp.int32, (vecs, 1), 0)
    for k in range(vecs):
        scale = lax.rsqrt(table[k : k + 1, k : k + 1])
        column = table[:, k : k + 1] * scale
        table_row = table[k : k + 1] * scale
        solved_row = solved[k : k + 1] * scale
        below = row_index > k
        at = row_index == k
        column = jnp.where(below, column, 0.0)
        table = table - column * table_row
        solved = jnp.where(at, solved_row, solved - column * solved_row)
    out_ref[...] = math.sqrt(samples) * solved


def whole(*shape_types):
    outs = tuple(jax.ShapeDtypeStruct(s, t) for s, t in shape_types)
    return outs if len(outs) > 1 else outs[0]


def local_call(body, outs, name, cost, args, grant=4):
    vmem = pl.BlockSpec(memory_space=pltpu.VMEM)
    return pl.pallas_call(
        body,
        out_shape=outs,
        name=name,
        in_specs=[vmem] * args,
        out_specs=jax.tree.map(lambda _: vmem, outs),
        compiler_params=pltpu.CompilerParams(vmem_limit_bytes=grant << 20),
        cost_estimate=pl.CostEstimate(flops=cost, bytes_accessed=cost // 64, transcendentals=0),
    )


def per_device(rows, cols, descriptors, densities, vectors):
    feat, count = descriptors.shape
    vecs = vectors.shape[0]
    samples = float(count * rows * cols)
    devices = rows * cols

    def swap(x, mask):
        return lax.ppermute(x, both_axes, [(i, i ^ mask) for i in range(devices)])

    core_mask = cols
    col_masks = [1 << b for b in range(int(math.log2(cols)))]
    row_masks = [cols << b for b in range(1, int(math.log2(rows)))]
    width = 2 * (count // 3)
    height = 2 * feat + vecs + pad_rows

    other_desc = swap(descriptors, core_mask)
    packed = local_call(pack_kernel, whole(((height, width), bf16)), "pack", 1 << 16, 3)(
        descriptors, densities[None, :], vectors
    )[None]
    for mask in col_masks[::-1] + row_masks:
        packed = jnp.concatenate([packed, swap(packed, mask)], axis=0)
    part = ((vecs + 8, count), f32)
    own, other = local_call(
        functools.partial(sums_kernel, vecs=vecs), whole(part, part), "sums", 1 << 30, 3, 16
    )(packed, descriptors, other_desc)
    got = swap(other, core_mask)
    diffused, grams = local_call(
        gram_kernel,
        whole(((vecs, count), f32), ((3 * vecs // 4, 4 * vecs), f32)),
        "gram",
        1 << 20,
        3,
    )(own, got, vectors)
    for mask in [core_mask] + row_masks + col_masks:
        grams = grams + swap(grams, mask)
    return local_call(
        functools.partial(whiten_kernel, samples=samples),
        whole(((vecs, count), f32)),
        "whiten",
        1 << 20,
        3,
    )(grams, diffused, vectors)


def solution(mesh):
    rows, cols = mesh.shape["row"], mesh.shape["col"]
    return jax.shard_map(
        functools.partial(per_device, rows, cols),
        mesh=mesh,
        in_specs=(P(None, both_axes), P(both_axes), P(None, both_axes)),
        out_specs=P(None, both_axes),
        check_vma=False,
    )
```
